32 devices in a mesh: grp: 4 (over y, x), shd: 8 (over z, core).
Axes of the slice: x: 2, y: 2, z: 4, core: 2. Of those that a mesh axis runs over, the one named last changes fastest.
Arguments:
- cells_in: bfloat16 [65536, 227], P(('grp', 'shd')), may hold values from -6 to 6
- targets: bfloat16 [65536, 227], P(('grp', 'shd')), may hold values from -6 to 6
- cell_areas: int32 [65536], P(('grp', 'shd')), may hold values from 1 to 32
- cell_node: int32 [65536], P(('grp', 'shd')), may hold values from 0 to 127, as said below
- adjacency: int32 [128, 8], P(('grp', 'shd')), may hold values from 0 to 15, as said below
- step_count: int32 [1], replicated, may hold values from 1 to 20
- weight_in: float32 [227, 512], P(None, 'shd'), may hold values from -0.375 to 0.375
- weight_layer: float32 [2, 512, 3072], P(None, 'shd'), may hold values from -2.1213203 to 2.1213203, as said below
- weight_dec: float32 [512, 739], P('shd'), may hold values from -0.25 to 0.25
- norm_gains: float32 [5, 512], P(None, 'shd'), may hold values from 0.2 to 4.8
- moment_in: float32 [227, 512], P(None, 'shd'), may hold values from -0.0007324219 to 0.0007324219
- moment_layer: float32 [2, 512, 3072], P(None, 'shd'), may hold values from -0.0007324219 to 0.0007324219
- moment_dec: float32 [512, 739], P('shd'), may hold values from -0.0007324219 to 0.0007324219
- moment_gains: float32 [5, 512], P(None, 'shd'), may hold values from -0.0007324219 to 0.0007324219
- square_in: float32 [227, 512], P(None, 'shd'), may hold values from 1.9215566e-08 to 1.9215565e-07
- square_layer: float32 [2, 512, 3072], P(None, 'shd'), may hold values from 1.9215566e-08 to 1.9215565e-07
- square_dec: float32 [512, 739], P('shd'), may hold values from 1.9215566e-08 to 1.9215565e-07
- square_gains: float32 [5, 512], P(None, 'shd'), may hold values from 1.9215566e-08 to 1.9215565e-07
Outputs:
- loss_value: float32 [], replicated
- grad_norm: float32 [], replicated
- delta_in: float32 [227, 512], P(None, 'shd')
- delta_layer: float32 [2, 512, 3072], P(None, 'shd')
- delta_dec: float32 [512, 739], P('shd')
- delta_gains: float32 [5, 512], P(None, 'shd')
- first_in: float32 [227, 512], P(None, 'shd')
- first_layer: float32 [2, 512, 3072], P(None, 'shd')
- first_dec: float32 [512, 739], P('shd')
- first_gains: float32 [5, 512], P(None, 'shd')
- second_in: float32 [227, 512], P(None, 'shd')
- second_layer: float32 [2, 512, 3072], P(None, 'shd')
- second_dec: float32 [512, 739], P('shd')
- second_gains: float32 [5, 512], P(None, 'shd')
The draws below stay inside these ranges and needn't reach their ends.
Inputs may be any that keep to these rules, and one draw needn't show every extreme that they name: `cell_node`: within each aligned run of 512 cells every value occurs at least once; the run's cells belong to node block (run index) of the same device. `adjacency`: each row holds 8 distinct values. `weight_layer`: entries of the output block (columns 1536 up to 2048) lie within 8 times the bound of the other columns, which lie within 6 / sqrt(512).
All inputs are finite; a program needn't handle non-finite values.
Results may differ from the reference program's by a relative error of at most 0.028.
The reference program's roundings to bfloat16 on the way count: a program that leaves them out, or rounds other values in their place, can miss the bound.
Values may be sent and summed in bfloat16 or wider, within the bound.
No kernel may reach another device: no remote copies, remote signals or barrier semaphores. Data moves between devices by JAX's collectives and lax.ppermute only.
A program may use at most 256 MiB of HBM per device.

```python
import math
import jax
import jax.numpy as jnp
from jax import lax

D = 512
HEADS = 8
HEAD_DIM = 64
C_IN = 227
C_OUT = 227
BLOCK = 128
SOURCES = 8
RATIO = 4
LAYERS = 2
NODE_DEV = 512
NODES = 16384
CELLS = 65536
NODE_BLOCKS = 128
POOL_BLOCKS = 16
N_SHD = 8


def draw_weight_layer(key, part):
    raw_values = jnp.clip(jax.random.normal(key, (LAYERS, D, 6, D), jnp.float32), -6.0, 6.0)
    column_scale = jnp.array([1.0, 1.0, 1.0, 8.0, 1.0, 1.0], jnp.float32) * D ** (-0.5)
    return (raw_values * column_scale[None, None, :, None]).reshape(LAYERS, D, 6 * D)


def draw_norm_gains(key, part):
    key_noise = jax.random.fold_in(key, 41)
    position = jnp.arange(D, dtype=jnp.float32) / (D - 1.0)
    noise = 1.0 + 0.1 * jnp.clip(jax.random.normal(key_noise, (2 * LAYERS + 1, D), jnp.float32), -3.0, 3.0)
    base = 0.3 * jnp.power(10.0, position)
    return base[None, :] * noise


def draw_cell_areas(key, part):
    base = jax.random.randint(jax.random.fold_in(key, 31), (CELLS,), 1, 5).astype(jnp.int32)
    base = base.at[0].set(1).at[CELLS - 1].set(4)
    quarter = (jnp.arange(CELLS, dtype=jnp.int32) * 4 // CELLS).astype(jnp.int32)
    factor = jnp.array([1, 2, 4, 8], jnp.int32)[quarter]
    return (base * factor).astype(jnp.int32)


def draw_cell_node(key, part):
    key_first = jax.random.fold_in(key, 11)
    key_second = jax.random.fold_in(key, 12)
    run_count = CELLS // (RATIO * BLOCK)
    key_list = jax.random.split(key_first, run_count)
    covered = jax.vmap(lambda single: jax.random.permutation(single, BLOCK))(key_list).astype(jnp.int32)
    extra_nodes = jax.random.randint(key_second, (run_count, (RATIO - 1) * BLOCK), 0, BLOCK).astype(jnp.int32)
    return jnp.concatenate([covered, extra_nodes], axis=1).reshape(CELLS)


def draw_adjacency(key, part):
    key_list = jax.random.split(jax.random.fold_in(key, 21), NODE_BLOCKS)
    chosen = jax.vmap(lambda single: jax.random.permutation(single, POOL_BLOCKS)[:SOURCES])(key_list)
    return chosen.astype(jnp.int32)


def block_scale(rng, shape, shards, low, largest):
    gain = 1.0
    for dim, blocks in shards:
        heights = jax.random.uniform(jax.random.fold_in(jax.random.fold_in(rng, 6), dim), (blocks,), jnp.float32, low / len(shards), largest / len(shards))
        gain = gain * jnp.repeat(jnp.exp(heights), shape[dim] // blocks).reshape((-1,) + (1,) * (len(shape) - 1 - dim))
    return gain


def normal_values(rng, shape, spread, bound, cuts=(), held_as=jnp.bfloat16):
    drawn = spread * jax.random.normal(rng, shape, jnp.float32)
    if cuts:
        drawn = drawn * block_scale(rng, shape, cuts, -0.22, 0.18)
    return jnp.clip(drawn, -bound, bound).astype(held_as)


def setup_inputs(seed: int = 0) -> dict:
    arg_keys = jax.random.split(jax.random.key(seed), 19)
    return {
        "cells_in": normal_values(arg_keys[0], (CELLS, C_IN), 1.0, 6.0, ((0, 32),)),
        "targets": normal_values(arg_keys[1], (CELLS, C_OUT), 1.0, 6.0, ((0, 32),)),
        "cell_areas": draw_cell_areas(jax.random.fold_in(arg_keys[18], 71), 0),
        "cell_node": draw_cell_node(jax.random.fold_in(arg_keys[18], 71), 0),
        "adjacency": draw_adjacency(jax.random.fold_in(arg_keys[18], 71), 0),
        "step_count": jax.random.randint(arg_keys[5], (1,), 1, 21).astype(jnp.int32),
        "weight_in": normal_values(arg_keys[6], (C_IN, D), C_IN ** -0.5, 0.375, ((1, 8),), jnp.float32),
        "weight_layer": draw_weight_layer(jax.random.fold_in(arg_keys[18], 71), 0),
        "weight_dec": normal_values(arg_keys[8], (D, D + C_OUT), D ** -0.5, 0.25, ((0, 8),), jnp.float32),
        "norm_gains": draw_norm_gains(jax.random.fold_in(arg_keys[18], 71), 0),
        "moment_in": normal_values(arg_keys[10], (C_IN, D), (0.22 * (C_IN * D + 6 * LAYERS * D * D + D * (D + C_OUT) + (2 * LAYERS + 1) * D) ** -0.5), 0.0007324219, ((1, 8),), jnp.float32),
        "moment_layer": normal_values(arg_keys[11], (LAYERS, D, 6 * D), (0.22 * (C_IN * D + 6 * LAYERS * D * D + D * (D + C_OUT) + (2 * LAYERS + 1) * D) ** -0.5), 0.0007324219, ((1, 8),), jnp.float32),
        "moment_dec": normal_values(arg_keys[12], (D, D + C_OUT), (0.22 * (C_IN * D + 6 * LAYERS * D * D + D * (D + C_OUT) + (2 * LAYERS + 1) * D) ** -0.5), 0.0007324219, ((0, 8),), jnp.float32),
        "moment_gains": normal_values(arg_keys[13], (2 * LAYERS + 1, D), (0.22 * (C_IN * D + 6 * LAYERS * D * D + D * (D + C_OUT) + (2 * LAYERS + 1) * D) ** -0.5), 0.0007324219, ((1, 8),), jnp.float32),
        "square_in": jnp.clip(jnp.exp(math.log(1.9215565316699212e-07) - 2.3025851 * jax.random.uniform(arg_keys[14], (C_IN, D), jnp.float32) ** block_scale(arg_keys[14], (C_IN, D), ((1, 8),), -0.2, 0.2)), 1.9215566027241948e-08, 1.9215565316699212e-07),
        "square_layer": jnp.clip(jnp.exp(math.log(1.9215565316699212e-07) - 2.3025851 * jax.random.uniform(arg_keys[15], (LAYERS, D, 6 * D), jnp.float32) ** block_scale(arg_keys[15], (LAYERS, D, 6 * D), ((1, 8),), -0.2, 0.2)), 1.9215566027241948e-08, 1.9215565316699212e-07),
        "square_dec": jnp.clip(jnp.exp(math.log(1.9215565316699212e-07) - 2.3025851 * jax.random.uniform(arg_keys[16], (D, D + C_OUT), jnp.float32) ** block_scale(arg_keys[16], (D, D + C_OUT), ((0, 8),), -0.2, 0.2)), 1.9215566027241948e-08, 1.9215565316699212e-07),
        "square_gains": jnp.clip(jnp.exp(math.log(1.9215565316699212e-07) - 2.3025851 * jax.random.uniform(arg_keys[17], (2 * LAYERS + 1, D), jnp.float32) ** block_scale(arg_keys[17], (2 * LAYERS + 1, D), ((1, 8),), -0.2, 0.2)), 1.9215566027241948e-08, 1.9215565316699212e-07),
    }


@jax.custom_vjp
def low(v):
    return lax.optimization_barrier(v.astype(jnp.bfloat16)).astype(jnp.float32)

@jax.custom_vjp
def low_back(v):
    return v

def low_keep(v):
    return (low(v), None)

def low_pass(kept, grad):
    return (grad,)

def back_keep(v):
    return (v, None)

def back_low(kept, grad):
    return (low(grad),)
low.defvjp(low_keep, low_pass)
low_back.defvjp(back_keep, back_low)
HIGH = lax.Precision.HIGHEST
eps_norm = 1e-05
score_scale = 0.125
clip_limit = 2.0
learn_rate = 0.02
decay_coef = 0.1
beta_one = 0.9
beta_two = 0.95
adam_eps = 1e-08

def matmul(left, right):
    return jnp.dot(left, right, precision=HIGH, preferred_element_type=jnp.float32)

def layer_norm(values, gain_row):
    average = lax.optimization_barrier(jnp.mean(values, axis=-1, keepdims=True))
    centered = values - average
    variance = lax.optimization_barrier(jnp.mean(centered * centered, axis=-1, keepdims=True))
    return centered * lax.rsqrt(variance + eps_norm) * gain_row

def attend_group(query_grp, key_grp, value_grp):
    scores = jnp.einsum('gqhd,gkhd->ghqk', query_grp, key_grp, precision=HIGH) * score_scale
    scores = low_back(scores)
    probs = jax.nn.softmax(scores, axis=-1)
    return jnp.einsum('ghqk,gkhd->gqhd', low(probs), value_grp, precision=HIGH)

def attention(queries, keys, values, adjacency):
    local_blocks = NODE_DEV // BLOCK
    group_size = math.gcd(4, local_blocks)
    block_ids = jnp.arange(NODE_BLOCKS, dtype=jnp.int32)
    shard_ids = block_ids // local_blocks % N_SHD
    source_group = adjacency.astype(jnp.int32) // local_blocks
    source_local = adjacency.astype(jnp.int32) % local_blocks
    sources = ((source_group * N_SHD + shard_ids[:, None]) * local_blocks + source_local).astype(jnp.int32)
    query_groups = queries.reshape(NODE_BLOCKS // group_size, group_size, BLOCK, HEADS, HEAD_DIM)
    source_groups = sources.reshape(NODE_BLOCKS // group_size, group_size, SOURCES)
    key_blocks = keys.reshape(NODE_BLOCKS, BLOCK, HEADS, HEAD_DIM)
    value_blocks = values.reshape(NODE_BLOCKS, BLOCK, HEADS, HEAD_DIM)

    def one_group(group_items):
        query_grp, picked = group_items
        key_grp = key_blocks[picked].reshape(group_size, SOURCES * BLOCK, HEADS, HEAD_DIM)
        value_grp = value_blocks[picked].reshape(group_size, SOURCES * BLOCK, HEADS, HEAD_DIM)
        return attend_group(query_grp, key_grp, value_grp)
    outputs = lax.map(jax.checkpoint(one_group), (query_groups, source_groups))
    return outputs.reshape(NODES, D)

def forward(weight_in, weight_layer, weight_dec, norm_gains, cells_f, targets_f, areas_f, cell_node, adjacency, area_total):
    low_in = low(weight_in)
    low_layer = low(weight_layer)
    low_dec = low(weight_dec)
    gain_all = low(norm_gains)
    encoded = low_back(low(matmul(cells_f, low_in)))
    node_ids = (jnp.arange(CELLS, dtype=jnp.int32) // (RATIO * BLOCK) * BLOCK + cell_node.astype(jnp.int32)).astype(jnp.int32)
    summed = low_back(jax.ops.segment_sum(encoded, node_ids, num_segments=NODES))
    counts = jax.ops.segment_sum(jnp.ones((CELLS,), jnp.float32), node_ids, num_segments=NODES)
    hidden = summed / counts[:, None]
    for layer_idx in range(LAYERS):
        matrices = low_layer[layer_idx]
        normed_one = low(layer_norm(hidden, gain_all[2 * layer_idx]))
        projected = low_back(low(matmul(normed_one, matrices[:, :3 * D])))
        attended = attention(projected[:, :D], projected[:, D:2 * D], projected[:, 2 * D:], adjacency)
        attended = low_back(low(attended))
        hidden = hidden + low_back(matmul(attended, matrices[:, 3 * D:4 * D]))
        normed_two = low(layer_norm(hidden, gain_all[2 * layer_idx + 1]))
        inner_up = low_back(matmul(normed_two, matrices[:, 4 * D:5 * D]))
        activated = low(jax.nn.silu(inner_up))
        hidden = hidden + low_back(matmul(activated, matrices[:, 5 * D:]))
    node_low = low(hidden)
    combined = low_back(encoded + node_low[node_ids])
    normed_dec = low(layer_norm(combined, gain_all[2 * LAYERS]))
    inner_dec = low_back(matmul(normed_dec, low_dec[:, :D]))
    activated_dec = low(jax.nn.silu(inner_dec))
    predicted = low_back(matmul(activated_dec, low_dec[:, D:]))
    errors = predicted - targets_f
    return jnp.sum(areas_f[:, None] * errors * errors) / area_total

def reference(cells_in, targets, cell_areas, cell_node, adjacency, step_count, weight_in, weight_layer, weight_dec, norm_gains, moment_in, moment_layer, moment_dec, moment_gains, square_in, square_layer, square_dec, square_gains):
    cells_f = cells_in.astype(jnp.float32)
    targets_f = targets.astype(jnp.float32)
    areas_f = cell_areas.astype(jnp.float32)
    area_total = jnp.sum(areas_f)

    def loss_of(first_weight, second_weight, third_weight, gain_weight):
        return forward(first_weight, second_weight, third_weight, gain_weight, cells_f, targets_f, areas_f, cell_node, adjacency, area_total)
    loss_value, pullback = jax.vjp(loss_of, weight_in, weight_layer, weight_dec, norm_gains)
    gradients = pullback(jnp.ones((), jnp.float32))
    squares = jnp.float32(0.0)
    for gradient in gradients:
        squares = squares + jnp.sum(gradient * gradient)
    grad_norm = jnp.sqrt(squares)
    factor = clip_limit / jnp.maximum(grad_norm, clip_limit)
    step_value = step_count[0].astype(jnp.float32)
    first_fix = 1.0 - jnp.power(jnp.float32(beta_one), step_value)
    second_fix = 1.0 - jnp.power(jnp.float32(beta_two), step_value)
    weights = (weight_in, weight_layer, weight_dec, norm_gains)
    moments = (moment_in, moment_layer, moment_dec, moment_gains)
    squared = (square_in, square_layer, square_dec, square_gains)
    decays = (decay_coef, decay_coef, decay_coef, 0.0)
    deltas, firsts, seconds = ([], [], [])
    for index_w in range(4):
        clipped = gradients[index_w] * factor
        first = beta_one * moments[index_w] + (1.0 - beta_one) * clipped
        second = beta_two * squared[index_w] + (1.0 - beta_two) * clipped * clipped
        delta = -learn_rate * (first / first_fix / (jnp.sqrt(second / second_fix) + adam_eps) + decays[index_w] * weights[index_w])
        deltas.append(delta)
        firsts.append(first)
        seconds.append(second)
    return (loss_value, grad_norm, deltas[0], deltas[1], deltas[2], deltas[3], firsts[0], firsts[1], firsts[2], firsts[3], seconds[0], seconds[1], seconds[2], seconds[3])
```

```python
import functools
import math

import jax
import jax.numpy as jnp
from jax import lax
from jax.experimental import pallas as pl
from jax.experimental.pallas import tpu as pltpu
from jax.sharding import PartitionSpec as P

D = 512
HEADS = 8
HEAD_DIM = 64
BLOCK = 128
SOURCES = 8
RATIO = 4
LAYERS = 2
CELL_BLOCK = RATIO * BLOCK
PICKED = SOURCES * BLOCK
LANES = 256
PACK = LANES // HEAD_DIM

eps_norm = 1e-05
score_scale = 0.125
clip_limit = 2.0
learn_rate = 0.02
decay_coef = 0.1
beta_one = 0.9
beta_two = 0.95
adam_eps = 1e-08

f32 = jnp.float32
bf16 = jnp.bfloat16
VMEM_LIMIT = 58 * 1024 * 1024


def nn(left, right):
    return jnp.dot(left, right, preferred_element_type=f32)


def tn(left, right):
    return lax.dot_general(left, right, (((0,), (0,)), ((), ())), preferred_element_type=f32)


def nt(left, right):
    return lax.dot_general(left, right, (((1,), (1,)), ((), ())), preferred_element_type=f32)


def norm_parts(values):
    average = jnp.mean(values, axis=-1, keepdims=True)
    centered = values - average
    variance = jnp.mean(centered * centered, axis=-1, keepdims=True)
    inverse = lax.rsqrt(variance + eps_norm)
    return (centered * inverse, inverse)


def norm_back(grad_out, normal, inverse, gain_row):
    grad_normal = grad_out * gain_row
    grad_gain = jnp.sum(grad_out * normal, axis=0, keepdims=True)
    mean_first = jnp.mean(grad_normal, axis=-1, keepdims=True)
    mean_second = jnp.mean(grad_normal * normal, axis=-1, keepdims=True)
    return (inverse * (grad_normal - mean_first - normal * mean_second), grad_gain)


def sigmoid(values):
    return 1.0 / (1.0 + jnp.exp(-values))


def node_match(node_row):
    rows = lax.broadcasted_iota(jnp.int32, (BLOCK, CELL_BLOCK), 0)
    return (rows == node_row).astype(f32)


def to_column(row):
    return jnp.transpose(jnp.broadcast_to(row, (BLOCK, row.shape[1])))[:, :1]


def spread_heads(rows):
    head = lax.broadcasted_iota(jnp.int32, rows.shape, 1) // HEAD_DIM
    zero = jnp.zeros_like(rows)
    return jnp.concatenate([jnp.where(head == h, rows, zero) for h in range(PACK)], axis=0)


def gather_heads(stacked):
    head = lax.broadcasted_iota(jnp.int32, (BLOCK, LANES), 1) // HEAD_DIM
    result = jnp.zeros((BLOCK, LANES), stacked.dtype)
    for h in range(PACK):
        result = jnp.where(head == h, stacked[h * BLOCK : (h + 1) * BLOCK], result)
    return result


def whole(memory_space=pltpu.VMEM):
    return pl.BlockSpec(memory_space=memory_space)


def call(body, out_shape, in_specs, scratch=(), flops=0, name=None, **kw):
    return pl.pallas_call(
        body,
        out_shape=out_shape,
        in_specs=in_specs,
        scratch_shapes=scratch,
        compiler_params=pltpu.CompilerParams(vmem_limit_bytes=VMEM_LIMIT),
        cost_estimate=pl.CostEstimate(flops=flops, bytes_accessed=8 << 20, transcendentals=0),
        name=name,
        **kw,
    )


def encode_body(cells_ref, node_ref, weight_ref, gain_ref, enc_ref, hidden_ref, normed_ref, count_ref):
    encoded = nn(cells_ref[...], weight_ref[...]).astype(bf16)
    enc_ref[...] = encoded
    match = node_match(node_ref[0])
    counts = jnp.sum(match, axis=1, keepdims=True)
    hidden = nn(match.astype(bf16), encoded) / counts
    hidden_ref[...] = hidden
    normal, _ = norm_parts(hidden)
    normed_ref[...] = (normal * gain_ref[0:1, :]).astype(bf16)
    count_ref[...] = jnp.broadcast_to(counts, (BLOCK, BLOCK))


def encode(cells, node, weight, gains):
    blocks = cells.shape[0] // CELL_BLOCK
    nodes = blocks * BLOCK
    row_spec = lambda rows, cols: pl.BlockSpec((rows, cols), lambda i: (i, 0))
    fixed = lambda a: pl.BlockSpec(a.shape, lambda i: (0,) * a.ndim)
    return pl.pallas_call(
        encode_body,
        grid=(blocks,),
        out_shape=(
            jax.ShapeDtypeStruct((cells.shape[0], D), bf16),
            jax.ShapeDtypeStruct((nodes, D), f32),
            jax.ShapeDtypeStruct((nodes, D), bf16),
            jax.ShapeDtypeStruct((nodes, BLOCK), f32),
        ),
        in_specs=[
            row_spec(CELL_BLOCK, cells.shape[1]),
            pl.BlockSpec((1, 1, CELL_BLOCK), lambda i: (i, 0, 0)),
            fixed(weight),
            fixed(gains),
        ],
        out_specs=(row_spec(CELL_BLOCK, D), row_spec(BLOCK, D), row_spec(BLOCK, D), row_spec(BLOCK, BLOCK)),
        compiler_params=pltpu.CompilerParams(vmem_limit_bytes=VMEM_LIMIT),
        cost_estimate=pl.CostEstimate(flops=10**9, bytes_accessed=6 << 20, transcendentals=0),
        name="encode",
    )(cells, node, weight, gains)


def layer_forward_body(
    layer, parts, adj_ref, own_ref, *refs
):
    part_refs = refs[:parts]
    h_ref, w_ref, gain_ref = refs[parts : parts + 3]
    next_ref, mid_ref, att_ref, normed_ref, q_ref, k_ref, v_ref, lse_ref = refs[parts + 3 : parts + 11]
    kg, vg = refs[parts + 11 :]
    start = 0
    for part in part_refs:
        rows = part.shape[0]
        for first in range(0, rows, 512):
            step = min(512, rows - first)
            block = part[first : first + step, :]
            k_ref[start : start + step, :] = nn(block, w_ref[:, D : 2 * D]).astype(bf16)
            v_ref[start : start + step, :] = nn(block, w_ref[:, 2 * D : 3 * D]).astype(bf16)
            start += step
    q_ref[...] = nn(own_ref[...], w_ref[:, :D]).astype(bf16)
    blocks = own_ref.shape[0] // BLOCK

    def one_block(r, _):
        rows = pl.ds(pl.multiple_of(r * BLOCK, BLOCK), BLOCK)
        for j in range(SOURCES):
            source = pl.ds(pl.multiple_of(adj_ref[r * SOURCES + j] * BLOCK, BLOCK), BLOCK)
            kg[j * BLOCK : (j + 1) * BLOCK, :] = k_ref[source, :]
            vg[j * BLOCK : (j + 1) * BLOCK, :] = v_ref[source, :]
        for g in range(D // LANES):
            lanes = slice(g * LANES, (g + 1) * LANES)
            query = spread_heads(q_ref[rows, lanes] * jnp.asarray(score_scale, bf16))
            scores = nt(query, kg[:, lanes])
            largest = jnp.max(scores, axis=-1, keepdims=True)
            exponent = jnp.exp(scores - largest)
            total = jnp.sum(exponent, axis=-1, keepdims=True)
            probs = (exponent * (1.0 / total)).astype(bf16)
            out = nn(probs, vg[:, lanes])
            att_ref[rows, lanes] = gather_heads(out).astype(bf16)
            log_sum = jnp.broadcast_to(largest + jnp.log(total), (PACK * BLOCK, BLOCK))
            lse_ref[r, g] = jnp.transpose(log_sum)[0:8, :]
        return 0

    lax.fori_loop(0, blocks, one_block, 0)
    middle = h_ref[...] + nn(att_ref[...], w_ref[:, 3 * D : 4 * D])
    mid_ref[...] = middle
    normal, _ = norm_parts(middle)
    normed = (normal * gain_ref[2 * layer + 1 : 2 * layer + 2, :]).astype(bf16)
    inner = nn(normed, w_ref[:, 4 * D : 5 * D])
    activated = (inner * sigmoid(inner)).astype(bf16)
    hidden = middle + nn(activated, w_ref[:, 5 * D :])
    next_ref[...] = hidden
    normal, _ = norm_parts(hidden)
    normed_ref[...] = (normal * gain_ref[2 * layer + 2 : 2 * layer + 3, :]).astype(bf16)


def layer_forward(layer, own, parts, adj, hidden, weights, gains):
    nodes = own.shape[0]
    blocks = nodes // BLOCK
    pool = sum(p.shape[0] for p in parts)
    sds = jax.ShapeDtypeStruct
    return call(
        functools.partial(layer_forward_body, layer, len(parts)),
        (
            sds((nodes, D), f32),
            sds((nodes, D), f32),
            sds((nodes, D), bf16),
            sds((nodes, D), bf16),
            sds((nodes, D), bf16),
            sds((pool, D), bf16),
            sds((pool, D), bf16),
            sds((blocks, D // LANES, 8, PACK * BLOCK), f32),
        ),
        [whole(pltpu.SMEM)] + [whole()] * (len(parts) + 4),
        scratch=(pltpu.VMEM((PICKED, D), bf16), pltpu.VMEM((PICKED, D), bf16)),
        flops=6 * 10**9,
        name=f"layer_forward_{layer}",
    )(adj, own, *parts, hidden, weights, gains)


def decode_body(
    inv_ref, enc_ref, node_ref, hidden_ref, area_ref, target_ref, w_ref, gain_ref,
    loss_ref, gcomb_ref, ghid_ref, gin_ref, gout_ref, ggain_ref,
):
    step = pl.program_id(0)
    match = node_match(node_ref[0]).astype(bf16)
    spread = tn(match, hidden_ref[...].astype(bf16))
    combined = enc_ref[...].astype(f32) + spread
    normal, inverse = norm_parts(combined)
    gain = gain_ref[2 * LAYERS : 2 * LAYERS + 1, :]
    normed = (normal * gain).astype(bf16)
    inner = nn(normed, w_ref[:, :D])
    sigma = sigmoid(inner)
    activated = (inner * sigma).astype(bf16)
    predicted = nn(activated, w_ref[:, D:])
    errors = predicted - target_ref[...].astype(f32)
    weighted = to_column(area_ref[0].astype(f32)) * errors
    part = jnp.sum(weighted * errors) * inv_ref[0]
    grad_pred = (2.0 * weighted * inv_ref[0]).astype(bf16)
    grad_out = tn(activated, grad_pred)
    grad_act = nt(grad_pred, w_ref[:, D:])
    grad_inner = (grad_act * (sigma * (1.0 + inner * (1.0 - sigma)))).astype(bf16)
    grad_in = tn(normed, grad_inner)
    grad_normed = nt(grad_inner, w_ref[:, :D])
    grad_comb, grad_gain = norm_back(grad_normed, normal, inverse, gain)
    grad_comb = grad_comb.astype(bf16)
    gcomb_ref[...] = grad_comb
    ghid_ref[...] = nn(match, grad_comb)

    @pl.when(step == 0)
    def _():
        loss_ref[0, 0] = part
        gin_ref[...] = grad_in
        gout_ref[...] = grad_out
        ggain_ref[...] = grad_gain

    @pl.when(step > 0)
    def _():
        loss_ref[0, 0] += part
        gin_ref[...] += grad_in
        gout_ref[...] += grad_out
        ggain_ref[...] += grad_gain


def decode(inv_area, encoded, node, hidden, areas, targets, weights, gains):
    blocks = encoded.shape[0] // CELL_BLOCK
    c_out = targets.shape[1]
    row_spec = lambda rows, cols: pl.BlockSpec((rows, cols), lambda i: (i, 0))
    fixed = lambda shape: pl.BlockSpec(shape, lambda i: (0,) * len(shape))
    line = pl.BlockSpec((1, 1, CELL_BLOCK), lambda i: (i, 0, 0))
    sds = jax.ShapeDtypeStruct
    return pl.pallas_call(
        decode_body,
        grid=(blocks,),
        out_shape=(
            sds((1, 1), f32),
            sds(encoded.shape, bf16),
            sds(hidden.shape, f32),
            sds((D, D), f32),
            sds((D, c_out), f32),
            sds((1, D), f32),
        ),
        in_specs=[
            whole(pltpu.SMEM),
            row_spec(CELL_BLOCK, D),
            line,
            row_spec(BLOCK, D),
            line,
            row_spec(CELL_BLOCK, c_out),
            fixed(weights.shape),
            fixed(gains.shape),
        ],
        out_specs=(
            pl.BlockSpec((1, 1), lambda i: (0, 0), memory_space=pltpu.SMEM),
            row_spec(CELL_BLOCK, D),
            row_spec(BLOCK, D),
            fixed((D, D)),
            fixed((D, c_out)),
            fixed((1, D)),
        ),
        compiler_params=pltpu.CompilerParams(vmem_limit_bytes=VMEM_LIMIT),
        cost_estimate=pl.CostEstimate(flops=5 * 10**9, bytes_accessed=8 << 20, transcendentals=0),
        name="decode",
    )(inv_area, encoded, node, hidden, areas, targets, weights, gains)


def first_norm_back(layer, gmid, grad_normed, hidden, gain_ref):
    normal, inverse = norm_parts(hidden)
    grad_first, grad_gain = norm_back(grad_normed, normal, inverse, gain_ref[2 * layer : 2 * layer + 1, :])
    return gmid + grad_first, grad_gain


def layer_backward_body(layer, above, adj_ref, *refs):
    refs = list(refs)
    take = lambda count: [refs.pop(0) for _ in range(count)]
    if above is None:
        (gh_ref,) = take(1)
    else:
        gmid_above, gown_above, habove_ref = take(3)
        received = take(above)
    mid_ref, att_ref, q_ref, k_ref, v_ref, lse_ref, w_ref, gain_ref = take(8)
    gmid_ref, gq_ref, gk_ref, gv_ref, gpool_ref, grest_ref, ggain_ref = take(7)
    if above is not None:
        (ggain_above_ref,) = take(1)
    kg, vg, gatt_ref, dk, dv = refs
    if above is None:
        grad_hidden = gh_ref[...]
    else:
        grad_normed = gown_above[...]
        for part in received:
            grad_normed = grad_normed + part[...].astype(f32)
        grad_hidden, ggain_above_ref[...] = first_norm_back(
            layer + 1, gmid_above[...], grad_normed, habove_ref[...], gain_ref
        )
    low = grad_hidden.astype(bf16)
    normal, inverse = norm_parts(mid_ref[...])
    gain = gain_ref[2 * layer + 1 : 2 * layer + 2, :]
    normed = (normal * gain).astype(bf16)
    inner = nn(normed, w_ref[:, 4 * D : 5 * D])
    sigma = sigmoid(inner)
    activated = (inner * sigma).astype(bf16)
    grest_ref[:, 2 * D :] = tn(activated, low).astype(bf16)
    grad_act = nt(low, w_ref[:, 5 * D :])
    grad_inner = (grad_act * (sigma * (1.0 + inner * (1.0 - sigma)))).astype(bf16)
    grest_ref[:, D : 2 * D] = tn(normed, grad_inner).astype(bf16)
    grad_normed = nt(grad_inner, w_ref[:, 4 * D : 5 * D])
    grad_mid, ggain_ref[...] = norm_back(grad_normed, normal, inverse, gain)
    grad_mid = grad_hidden + grad_mid
    gmid_ref[...] = grad_mid
    branch = grad_mid.astype(bf16)
    grest_ref[:, :D] = tn(att_ref[...], branch).astype(bf16)
    gatt_ref[...] = nt(branch, w_ref[:, 3 * D : 4 * D]).astype(bf16)
    dk[...] = jnp.zeros_like(dk)
    dv[...] = jnp.zeros_like(dv)
    blocks = mid_ref.shape[0] // BLOCK

    def one_block(r, _):
        rows = pl.ds(pl.multiple_of(r * BLOCK, BLOCK), BLOCK)
        sources = [
            pl.ds(pl.multiple_of(adj_ref[r * SOURCES + j] * BLOCK, BLOCK), BLOCK) for j in range(SOURCES)
        ]
        for j in range(SOURCES):
            kg[j * BLOCK : (j + 1) * BLOCK, :] = k_ref[sources[j], :]
            vg[j * BLOCK : (j + 1) * BLOCK, :] = v_ref[sources[j], :]
        for g in range(D // LANES):
            lanes = slice(g * LANES, (g + 1) * LANES)
            query = spread_heads(q_ref[rows, lanes] * jnp.asarray(score_scale, bf16))
            grad_out = spread_heads(gatt_ref[rows, lanes])
            probs = jnp.exp(nt(kg[:, lanes], query) - lse_ref[r, g, 0:1, :])
            grad_probs = nt(vg[:, lanes], grad_out)
            inner_sum = jnp.sum(probs * grad_probs, axis=0, keepdims=True)
            grad_scores = (probs * (grad_probs - inner_sum)).astype(bf16)
            grad_value = nn(probs.astype(bf16), grad_out)
            grad_key = nn(grad_scores, query)
            grad_query = gather_heads(tn(grad_scores, kg[:, lanes])) * score_scale
            gq_ref[rows, lanes] = grad_query.astype(bf16)
            for j in range(SOURCES):
                dk[sources[j], lanes] += grad_key[j * BLOCK : (j + 1) * BLOCK]
                dv[sources[j], lanes] += grad_value[j * BLOCK : (j + 1) * BLOCK]
        return 0

    lax.fori_loop(0, blocks, one_block, 0)
    for first in range(0, dk.shape[0], 512):
        rows = slice(first, first + 512)
        grad_key = dk[rows, :].astype(bf16)
        grad_value = dv[rows, :].astype(bf16)
        gk_ref[rows, :] = grad_key
        gv_ref[rows, :] = grad_value
        gpool_ref[rows, :] = (
            nt(grad_key, w_ref[:, D : 2 * D]) + nt(grad_value, w_ref[:, 2 * D : 3 * D])
        ).astype(bf16)


def layer_backward(layer, above, adj, mid, att, q, k, v, lse, weights, gains):
    nodes = mid.shape[0]
    pool = k.shape[0]
    sds = jax.ShapeDtypeStruct
    outs = [
        sds((nodes, D), f32),
        sds((nodes, D), bf16),
        sds((pool, D), bf16),
        sds((pool, D), bf16),
        sds((pool, D), bf16),
        sds((D, 3 * D), bf16),
        sds((1, D), f32),
    ]
    count = None if len(above) == 1 else len(above) - 3
    if count is not None:
        outs.append(sds((1, D), f32))
    return call(
        functools.partial(layer_backward_body, layer, count),
        tuple(outs),
        [whole(pltpu.SMEM)] + [whole()] * (len(above) + 8),
        scratch=(
            pltpu.VMEM((PICKED, D), bf16),
            pltpu.VMEM((PICKED, D), bf16),
            pltpu.VMEM((nodes, D), bf16),
            pltpu.VMEM((pool, D), f32),
            pltpu.VMEM((pool, D), f32),
        ),
        flops=12 * 10**9,
        name=f"layer_backward_{layer}",
    )(adj, *above, mid, att, q, k, v, lse, weights, gains)


def projection_back_body(parts, own_ref, *refs):
    part_refs = refs[:parts]
    gq_ref, gk_ref, gv_ref, w_ref, gown_ref, gw_ref = refs[parts:]
    gown_ref[...] = nt(gq_ref[...], w_ref[:, :D])
    gw_ref[:, :D] = tn(own_ref[...], gq_ref[...]).astype(bf16)
    for index, source in ((1, gk_ref), (2, gv_ref)):
        total = None
        start = 0
        for part in part_refs:
            rows = part.shape[0]
            value = tn(part[...], source[start : start + rows, :])
            total = value if total is None else total + value
            start += rows
        gw_ref[:, index * D : (index + 1) * D] = total.astype(bf16)


def projection_back(layer, own, parts, gq, gk, gv, weights):
    sds = jax.ShapeDtypeStruct
    return call(
        functools.partial(projection_back_body, len(parts)),
        (sds((own.shape[0], D), f32), sds((D, 3 * D), bf16)),
        [whole()] * (len(parts) + 5),
        flops=3 * 10**9,
        name=f"projection_back_{layer}",
    )(own, *parts, gq, gk, gv, weights)


def encode_back_body(parts, *refs):
    gmid_ref, gown_ref, h_ref = refs[:3]
    received = refs[3 : 3 + parts]
    gain_ref, cells_ref, node_ref, gcomb_ref, count_ref, gin_ref, ggain_ref = refs[3 + parts :]
    step = pl.program_id(0)
    grad_normed = gown_ref[...]
    for part in received:
        grad_normed = grad_normed + part[...].astype(f32)
    grad_hidden, grad_gain = first_norm_back(0, gmid_ref[...], grad_normed, h_ref[...], gain_ref)
    summed = (grad_hidden / count_ref[:, :1]).astype(bf16)
    match = node_match(node_ref[0]).astype(bf16)
    grad_enc = (gcomb_ref[...].astype(f32) + tn(match, summed)).astype(bf16)
    grad_in = tn(grad_enc, cells_ref[...])

    @pl.when(step == 0)
    def _():
        gin_ref[...] = grad_in
        ggain_ref[...] = grad_gain

    @pl.when(step > 0)
    def _():
        gin_ref[...] += grad_in
        ggain_ref[...] += grad_gain


def encode_back(gmid, gown, hidden, received, gains, cells, node, gcomb, counts):
    blocks = cells.shape[0] // CELL_BLOCK
    row_spec = lambda rows, cols: pl.BlockSpec((rows, cols), lambda i: (i, 0))
    fixed = lambda shape: pl.BlockSpec(shape, lambda i: (0,) * len(shape))
    node_spec = row_spec(BLOCK, D)
    sds = jax.ShapeDtypeStruct
    return pl.pallas_call(
        functools.partial(encode_back_body, len(received)),
        grid=(blocks,),
        out_shape=(sds((D, cells.shape[1]), f32), sds((1, D), f32)),
        in_specs=[node_spec] * (3 + len(received))
        + [
            fixed(gains.shape),
            row_spec(CELL_BLOCK, cells.shape[1]),
            pl.BlockSpec((1, 1, CELL_BLOCK), lambda i: (i, 0, 0)),
            row_spec(CELL_BLOCK, D),
            row_spec(BLOCK, BLOCK),
        ],
        out_specs=(fixed((D, cells.shape[1])), fixed((1, D))),
        compiler_params=pltpu.CompilerParams(vmem_limit_bytes=VMEM_LIMIT),
        cost_estimate=pl.CostEstimate(flops=10**9, bytes_accessed=8 << 20, transcendentals=0),
        name="encode_back",
    )(gmid, gown, hidden, *received, gains, cells, node, gcomb, counts)


def adam_step(gradient, weight, moment, square, factor, first_fix, second_fix, weight_decay):
    clipped = gradient * factor
    first = beta_one * moment + (1.0 - beta_one) * clipped
    second = beta_two * square + (1.0 - beta_two) * clipped * clipped
    delta = -learn_rate * (
        first / first_fix / (jnp.sqrt(second / second_fix) + adam_eps) + weight_decay * weight
    )
    return (delta, first, second)


def local(
    cells_in,
    targets,
    cell_areas,
    cell_node,
    adjacency,
    step_count,
    weight_in,
    weight_layer,
    weight_dec,
    norm_gains,
    moment_in,
    moment_layer,
    moment_dec,
    moment_gains,
    square_in,
    square_layer,
    square_dec,
    square_gains,
):
    blocks = adjacency.shape[0]
    areas_f = cell_areas.astype(f32)
    area_total = lax.psum(jnp.sum(areas_f), ("grp", "shd"))
    inv_area = (1.0 / area_total).reshape(1)
    low_in = lax.all_gather(weight_in.astype(bf16), "shd", axis=1, tiled=True)
    low_gains = lax.all_gather(norm_gains.astype(bf16), "shd", axis=1, tiled=True)
    low_layer = [
        lax.all_gather(weight_layer[i].astype(bf16), "shd", axis=0, tiled=True) for i in range(LAYERS)
    ]
    low_dec = lax.all_gather(weight_dec.astype(bf16), "shd", axis=0, tiled=True)
    gains = low_gains.astype(f32)
    node = cell_node.reshape(blocks, 1, CELL_BLOCK)
    areas = cell_areas.reshape(blocks, 1, CELL_BLOCK)
    adj = adjacency.reshape(-1)
    encoded, hidden, normed, counts = encode(cells_in, node, low_in, gains)
    kept = []
    for layer in range(LAYERS):
        pool = lax.all_gather(normed, "grp", axis=0, tiled=True)
        out = layer_forward(layer, normed, [pool], adj, hidden, low_layer[layer], gains)
        kept.append((hidden, normed, pool) + tuple(out[1:3]) + tuple(out[4:]))
        hidden, normed = out[0], out[3]
    loss_part, gcomb, ghid, gdec_in, gdec_out, gain_dec = decode(
        inv_area, encoded, node, hidden, areas, targets, low_dec, gains
    )
    gain_grads = [None] * (2 * LAYERS + 1)
    gain_grads[2 * LAYERS] = gain_dec
    layer_grads = [None] * LAYERS
    above = (ghid,)
    for layer in reversed(range(LAYERS)):
        h_in, normed, pool, mid, att, q, k, v, lse = kept[layer]
        back = layer_backward(layer, above, adj, mid, att, q, k, v, lse, low_layer[layer], gains)
        gmid, gq, gk, gv, gpool, grest, gain_grads[2 * layer + 1] = back[:7]
        if len(back) > 7:
            gain_grads[2 * layer + 2] = back[7]
        received = lax.psum_scatter(gpool, "grp", scatter_dimension=0, tiled=True)
        gown, gqkv = projection_back(layer, normed, [pool], gq, gk, gv, low_layer[layer])
        above = (gmid, gown, h_in, received)
        layer_grads[layer] = jnp.concatenate([gqkv, grest], axis=1)
    gmid, gown, h_in, received = above
    grad_in, gain_grads[0] = encode_back(gmid, gown, h_in, [received], gains, cells_in, node, gcomb, counts)
    grad_gains = jnp.concatenate(gain_grads, axis=0).T
    pieces = (
        grad_in.astype(bf16),
        layer_grads[0],
        layer_grads[1],
        jnp.concatenate([gdec_in, gdec_out], axis=1).astype(bf16),
        grad_gains.astype(bf16),
    )
    shards = [
        lax.psum(lax.psum_scatter(p, "shd", scatter_dimension=0, tiled=True), "grp").astype(f32) for p in pieces
    ]
    loss_group = lax.psum(loss_part[0, 0], "grp")
    group_sums = (shards[0].T, jnp.stack(shards[1:3], axis=0), shards[3], shards[4].T)
    squares_part = f32(0.0)
    for index_w in range(4):
        squares_part = squares_part + jnp.sum(group_sums[index_w] * group_sums[index_w])
    total_squares, loss_value = lax.psum((squares_part, loss_group), "shd")
    grad_norm = jnp.sqrt(total_squares)
    factor = clip_limit / jnp.maximum(grad_norm, clip_limit)
    step_value = step_count[0].astype(f32)
    first_fix = 1.0 - jnp.power(f32(beta_one), step_value)
    second_fix = 1.0 - jnp.power(f32(beta_two), step_value)
    weights = (weight_in, weight_layer, weight_dec, norm_gains)
    moments = (moment_in, moment_layer, moment_dec, moment_gains)
    squared = (square_in, square_layer, square_dec, square_gains)
    decays = (decay_coef, decay_coef, decay_coef, 0.0)
    deltas, firsts, seconds = ([], [], [])
    for index_w in range(4):
        delta, first, second = adam_step(
            group_sums[index_w],
            weights[index_w],
            moments[index_w],
            squared[index_w],
            factor,
            first_fix,
            second_fix,
            decays[index_w],
        )
        deltas.append(delta)
        firsts.append(first)
        seconds.append(second)
    return (loss_value, grad_norm, *deltas, *firsts, *seconds)


def solution(mesh):
    rows = P(("grp", "shd"), None)
    flat = P(("grp", "shd"))
    params = (P(None, "shd"), P(None, "shd", None), P("shd", None), P(None, "shd"))
    return jax.shard_map(
        local,
        mesh=mesh,
        in_specs=(rows, rows, flat, flat, rows, P()) + params * 3,
        out_specs=(P(), P()) + params * 3,
        check_vma=False,
    )
```

```python
import functools
import math

import jax
import jax.numpy as jnp
from jax import lax
from jax.experimental import pallas as pl
from jax.experimental.pallas import tpu as pltpu
from jax.sharding import PartitionSpec as P

D = 512
HEADS = 8
HEAD_DIM = 64
BLOCK = 128
SOURCES = 8
RATIO = 4
LAYERS = 2
CELL_BLOCK = RATIO * BLOCK
PICKED = SOURCES * BLOCK
LANES = 256
PACK = LANES // HEAD_DIM

eps_norm = 1e-05
score_scale = 0.125
clip_limit = 2.0
learn_rate = 0.02
decay_coef = 0.1
beta_one = 0.9
beta_two = 0.95
adam_eps = 1e-08

f32 = jnp.float32
bf16 = jnp.bfloat16
VMEM_LIMIT = 58 * 1024 * 1024


def nn(left, right):
    return jnp.dot(left, right, preferred_element_type=f32)


def tn(left, right):
    return lax.dot_general(left, right, (((0,), (0,)), ((), ())), preferred_element_type=f32)


def nt(left, right):
    return lax.dot_general(left, right, (((1,), (1,)), ((), ())), preferred_element_type=f32)


def norm_parts(values):
    average = jnp.mean(values, axis=-1, keepdims=True)
    centered = values - average
    variance = jnp.mean(centered * centered, axis=-1, keepdims=True)
    inverse = lax.rsqrt(variance + eps_norm)
    return (centered * inverse, inverse)


def norm_back(grad_out, normal, inverse, gain_row):
    grad_normal = grad_out * gain_row
    grad_gain = jnp.sum(grad_out * normal, axis=0, keepdims=True)
    mean_first = jnp.mean(grad_normal, axis=-1, keepdims=True)
    mean_second = jnp.mean(grad_normal * normal, axis=-1, keepdims=True)
    return (inverse * (grad_normal - mean_first - normal * mean_second), grad_gain)


def sigmoid(values):
    return 1.0 / (1.0 + jnp.exp(-values))


def node_match(node_row):
    rows = lax.broadcasted_iota(jnp.int32, (BLOCK, CELL_BLOCK), 0)
    return (rows == node_row).astype(f32)


def to_column(row):
    return jnp.transpose(jnp.broadcast_to(row, (BLOCK, row.shape[1])))[:, :1]


def spread_heads(rows):
    head = lax.broadcasted_iota(jnp.int32, rows.shape, 1) // HEAD_DIM
    zero = jnp.zeros_like(rows)
    return jnp.concatenate([jnp.where(head == h, rows, zero) for h in range(PACK)], axis=0)


def gather_heads(stacked):
    head = lax.broadcasted_iota(jnp.int32, (BLOCK, LANES), 1) // HEAD_DIM
    result = jnp.zeros((BLOCK, LANES), stacked.dtype)
    for h in range(PACK):
        result = jnp.where(head == h, stacked[h * BLOCK : (h + 1) * BLOCK], result)
    return result


def whole(memory_space=pltpu.VMEM):
    return pl.BlockSpec(memory_space=memory_space)


ANYWHERE = pl.BlockSpec(memory_space=pl.ANY)
WIDTH_LAYER = 6 * D
WIDTH_TOP = 6 * D + 768
WIDTH_IN = 384
GAIN_AT = 256
AREA_AT = GAIN_AT + 2 * LAYERS + 1
SHARD_ROWS = 16


def fetch(pieces, target, sems, first_col=0):
    cols = target.shape[1]
    copies = []
    if len(pieces) > 1:
        member = lax.axis_index("shd")
        place, core = member // 2, member % 2
    for i, piece in enumerate(pieces):
        rows = piece.shape[0]
        start = 0
        if len(pieces) > 1:
            start = (((place + 4 - i // 2) % 4) * 2 + (core ^ (i % 2))) * rows
        copy = pltpu.make_async_copy(
            piece.at[:, pl.ds(first_col, cols)],
            target.at[pl.ds(pl.multiple_of(start, rows), rows), :],
            sems.at[i],
        )
        copy.start()
        copies.append(copy)
    return copies


def finish(copies):
    for copy in copies:
        copy.wait()


def emit(fast, source, keep, send, sems, first_col, rows, spots):
    cols = source.shape[1]
    half = spots // 2
    copies = []
    if fast:
        member, group = lax.axis_index("shd"), lax.axis_index("grp")
        place, core = member // 2, member % 2
    for i in range(spots):
        start = i * rows
        if fast:
            across = i % half
            if spots == 8:
                start = ((place + across) % 4) * 128 + (core ^ (i // half)) * 64
            else:
                start = ((place + across % 4) % 4) * 128 + (core ^ (i // half)) * 64 + (group ^ (across // 4)) * 16
        copy = pltpu.make_async_copy(
            source.at[pl.ds(pl.multiple_of(start, rows), rows), :],
            (keep if i < half else send).at[i % half, :, pl.ds(first_col, cols)],
            sems.at[i],
        )
        copy.start()
        copies.append(copy)
    return copies


def call(body, out_shape, in_specs, scratch=(), flops=0, name=None, **kw):
    return pl.pallas_call(
        body,
        out_shape=out_shape,
        in_specs=in_specs,
        scratch_shapes=scratch,
        compiler_params=pltpu.CompilerParams(vmem_limit_bytes=VMEM_LIMIT),
        cost_estimate=pl.CostEstimate(flops=flops, bytes_accessed=8 << 20, transcendentals=0),
        name=name,
        **kw,
    )


def encode_body(c_in, pieces, cells_ref, node_ref, *refs):
    piece_refs = refs[:pieces]
    enc_ref, hidden_ref, normed_ref, count_ref, gain_ref, area_ref = refs[pieces : pieces + 6]
    w_ref, sems = refs[pieces + 6 :]

    @pl.when(pl.program_id(0) == 0)
    def _():
        finish(fetch(piece_refs, w_ref, sems))
        side = jnp.transpose(w_ref[:, GAIN_AT:].astype(f32))
        gain_ref[...] = side[0:8, :]
        each = side[AREA_AT - GAIN_AT : AREA_AT - GAIN_AT + 2, :]
        high, low = jnp.sum(each[0:1, :]), jnp.sum(each[1:2, :])
        area_ref[0, 0] = (high * 256.0 + low) * (len(piece_refs) / D if pieces > 1 else 1.0 / D)

    encoded = nt(cells_ref[...], w_ref[:, :c_in]).astype(bf16)
    enc_ref[...] = encoded
    match = node_match(node_ref[0])
    counts = jnp.sum(match, axis=1, keepdims=True)
    hidden = nn(match.astype(bf16), encoded) / counts
    hidden_ref[...] = hidden
    normal, _ = norm_parts(hidden)
    normed_ref[...] = (normal * gain_ref[0:1, :]).astype(bf16)
    count_ref[...] = jnp.broadcast_to(counts, (BLOCK, BLOCK))


def encode(cells, node, pieces):
    blocks = cells.shape[0] // CELL_BLOCK
    nodes = blocks * BLOCK
    row_spec = lambda rows, cols: pl.BlockSpec((rows, cols), lambda i: (i, 0))
    return pl.pallas_call(
        functools.partial(encode_body, cells.shape[1], len(pieces)),
        grid=(blocks,),
        out_shape=(
            jax.ShapeDtypeStruct((cells.shape[0], D), bf16),
            jax.ShapeDtypeStruct((nodes, D), f32),
            jax.ShapeDtypeStruct((nodes, D), bf16),
            jax.ShapeDtypeStruct((nodes, BLOCK), f32),
            jax.ShapeDtypeStruct((8, D), f32),
            jax.ShapeDtypeStruct((1, 1), f32),
        ),
        in_specs=[
            row_spec(CELL_BLOCK, cells.shape[1]),
            pl.BlockSpec((1, 1, CELL_BLOCK), lambda i: (i, 0, 0)),
        ]
        + [ANYWHERE] * len(pieces),
        out_specs=(
            row_spec(CELL_BLOCK, D),
            row_spec(BLOCK, D),
            row_spec(BLOCK, D),
            row_spec(BLOCK, BLOCK),
            pl.BlockSpec((8, D), lambda i: (0, 0)),
            pl.BlockSpec((1, 1), lambda i: (0, 0), memory_space=pltpu.SMEM),
        ),
        scratch_shapes=(pltpu.VMEM((D, WIDTH_IN), bf16), pltpu.SemaphoreType.DMA((len(pieces),))),
        compiler_params=pltpu.CompilerParams(vmem_limit_bytes=VMEM_LIMIT),
        cost_estimate=pl.CostEstimate(flops=10**9, bytes_accessed=6 << 20, transcendentals=0),
        name="encode",
    )(cells, node, *pieces)


def layer_forward_body(layer, fast, parts, pieces, adj_ref, own_ref, *refs):
    refs = list(refs)
    take = lambda count: [refs.pop(0) for _ in range(count)]
    part_refs = take(parts)
    h_ref, gain_ref = take(2)
    piece_refs = take(pieces)
    next_ref, mid_ref, att_ref, normed_ref, q_ref, k_ref, v_ref, lse_ref = take(8)
    kg, vg, w_ref, sems = refs
    finish(fetch(piece_refs, w_ref, sems))
    start = 0
    for part in part_refs:
        rows = part.shape[0]
        for first in range(0, rows, 512):
            step = min(512, rows - first)
            block = part[first : first + step, :]
            k_ref[start : start + step, :] = nn(block, w_ref[:, D : 2 * D]).astype(bf16)
            v_ref[start : start + step, :] = nn(block, w_ref[:, 2 * D : 3 * D]).astype(bf16)
            start += step
    q_ref[...] = nn(own_ref[...], w_ref[:, :D]).astype(bf16)
    blocks = own_ref.shape[0] // BLOCK
    turn = lax.axis_index("grp") * blocks if fast else 0

    def one_block(r, _):
        rows = pl.ds(pl.multiple_of(r * BLOCK, BLOCK), BLOCK)
        for j in range(SOURCES):
            source = pl.ds(pl.multiple_of((adj_ref[r * SOURCES + j] ^ turn) * BLOCK, BLOCK), BLOCK)
            kg[j * BLOCK : (j + 1) * BLOCK, :] = k_ref[source, :]
            vg[j * BLOCK : (j + 1) * BLOCK, :] = v_ref[source, :]
        for g in range(D // LANES):
            lanes = slice(g * LANES, (g + 1) * LANES)
            query = spread_heads(q_ref[rows, lanes] * jnp.asarray(score_scale, bf16))
            scores = nt(query, kg[:, lanes])
            largest = jnp.max(scores, axis=-1, keepdims=True)
            exponent = jnp.exp(scores - largest)
            total = jnp.sum(exponent, axis=-1, keepdims=True)
            probs = (exponent * (1.0 / total)).astype(bf16)
            out = nn(probs, vg[:, lanes])
            att_ref[rows, lanes] = gather_heads(out).astype(bf16)
            log_sum = jnp.broadcast_to(largest + jnp.log(total), (PACK * BLOCK, BLOCK))
            lse_ref[r, g] = jnp.transpose(log_sum)[0:8, :]
        return 0

    lax.fori_loop(0, blocks, one_block, 0)
    middle = h_ref[...] + nn(att_ref[...], w_ref[:, 3 * D : 4 * D])
    mid_ref[...] = middle
    normal, _ = norm_parts(middle)
    normed = (normal * gain_ref[2 * layer + 1 : 2 * layer + 2, :]).astype(bf16)
    inner = nn(normed, w_ref[:, 4 * D : 5 * D])
    activated = (inner * sigmoid(inner)).astype(bf16)
    hidden = middle + nn(activated, w_ref[:, 5 * D :])
    next_ref[...] = hidden
    normal, _ = norm_parts(hidden)
    normed_ref[...] = (normal * gain_ref[2 * layer + 2 : 2 * layer + 3, :]).astype(bf16)


def layer_forward(layer, fast, own, parts, adj, hidden, pieces, gains):
    nodes = own.shape[0]
    blocks = nodes // BLOCK
    pool = sum(p.shape[0] for p in parts)
    sds = jax.ShapeDtypeStruct
    return call(
        functools.partial(layer_forward_body, layer, fast, len(parts), len(pieces)),
        (
            sds((nodes, D), f32),
            sds((nodes, D), f32),
            sds((nodes, D), bf16),
            sds((nodes, D), bf16),
            sds((nodes, D), bf16),
            sds((pool, D), bf16),
            sds((pool, D), bf16),
            sds((blocks, D // LANES, 8, PACK * BLOCK), f32),
        ),
        [whole(pltpu.SMEM)] + [whole()] * (len(parts) + 3) + [ANYWHERE] * len(pieces),
        scratch=(
            pltpu.VMEM((PICKED, D), bf16),
            pltpu.VMEM((PICKED, D), bf16),
            pltpu.VMEM((D, WIDTH_LAYER), bf16),
            pltpu.SemaphoreType.DMA((len(pieces),)),
        ),
        flops=6 * 10**9,
        name=f"layer_forward_{layer}",
    )(adj, own, *parts, hidden, gains, *pieces)


def decode_body(
    fast, pieces, inv_ref, enc_ref, node_ref, hidden_ref, area_ref, target_ref, gain_ref, *refs
):
    piece_refs = refs[:pieces]
    loss_ref, gcomb_ref, ghid_ref, ggain_ref, keep_ref, send_ref = refs[pieces : pieces + 6]
    w_ref, gw_ref, glow_ref, sems, out_sems = refs[pieces + 6 :]
    step = pl.program_id(0)
    c_out = target_ref.shape[1]

    @pl.when(step == 0)
    def _():
        finish(fetch(piece_refs, w_ref, sems, WIDTH_LAYER))

    match = node_match(node_ref[0]).astype(bf16)
    spread = tn(match, hidden_ref[...].astype(bf16))
    combined = enc_ref[...].astype(f32) + spread
    normal, inverse = norm_parts(combined)
    gain = gain_ref[2 * LAYERS : 2 * LAYERS + 1, :]
    normed = (normal * gain).astype(bf16)
    inner = nn(normed, w_ref[:, :D])
    sigma = sigmoid(inner)
    activated = (inner * sigma).astype(bf16)
    predicted = nn(activated, w_ref[:, D : D + c_out])
    errors = predicted - target_ref[...].astype(f32)
    weighted = to_column(area_ref[0].astype(f32)) * errors
    part = jnp.sum(weighted * errors) * inv_ref[0]
    grad_pred = (2.0 * weighted * inv_ref[0]).astype(bf16)
    grad_out = tn(activated, grad_pred)
    grad_act = nt(grad_pred, w_ref[:, D : D + c_out])
    grad_inner = (grad_act * (sigma * (1.0 + inner * (1.0 - sigma)))).astype(bf16)
    grad_in = tn(normed, grad_inner)
    grad_normed = nt(grad_inner, w_ref[:, :D])
    grad_comb, grad_gain = norm_back(grad_normed, normal, inverse, gain)
    grad_comb = grad_comb.astype(bf16)
    gcomb_ref[...] = grad_comb
    ghid_ref[...] = nn(match, grad_comb)

    @pl.when(step == 0)
    def _():
        loss_ref[0, 0] = part
        gw_ref[:, :D] = grad_in
        gw_ref[:, D : D + c_out] = grad_out
        ggain_ref[...] = grad_gain

    @pl.when(step > 0)
    def _():
        loss_ref[0, 0] += part
        gw_ref[:, :D] += grad_in
        gw_ref[:, D : D + c_out] += grad_out
        ggain_ref[...] += grad_gain

    @pl.when(step == pl.num_programs(0) - 1)
    def _():
        glow_ref[:, : D + c_out] = gw_ref[:, : D + c_out].astype(bf16)
        glow_ref[:, D + c_out :] = jnp.zeros((D, 768 - D - c_out), bf16)
        finish(emit(fast, glow_ref, keep_ref, send_ref, out_sems, WIDTH_LAYER, SHARD_ROWS, 32))


def decode(fast, inv_area, encoded, node, hidden, areas, targets, pieces, gains):
    blocks = encoded.shape[0] // CELL_BLOCK
    c_out = targets.shape[1]
    row_spec = lambda rows, cols: pl.BlockSpec((rows, cols), lambda i: (i, 0))
    fixed = lambda shape: pl.BlockSpec(shape, lambda i: (0,) * len(shape))
    line = pl.BlockSpec((1, 1, CELL_BLOCK), lambda i: (i, 0, 0))
    sds = jax.ShapeDtypeStruct
    return pl.pallas_call(
        functools.partial(decode_body, fast, len(pieces)),
        grid=(blocks,),
        out_shape=(
            sds((1, 1), f32),
            sds(encoded.shape, bf16),
            sds(hidden.shape, f32),
            sds((1, D), f32),
            sds((16, SHARD_ROWS, WIDTH_TOP), bf16),
            sds((16, SHARD_ROWS, WIDTH_TOP), bf16),
        ),
        in_specs=[
            whole(pltpu.SMEM),
            row_spec(CELL_BLOCK, D),
            line,
            row_spec(BLOCK, D),
            line,
            row_spec(CELL_BLOCK, c_out),
            fixed(gains.shape),
        ]
        + [ANYWHERE] * len(pieces),
        out_specs=(
            pl.BlockSpec((1, 1), lambda i: (0, 0), memory_space=pltpu.SMEM),
            row_spec(CELL_BLOCK, D),
            row_spec(BLOCK, D),
            fixed((1, D)),
            ANYWHERE,
            ANYWHERE,
        ),
        scratch_shapes=(
            pltpu.VMEM((D, 768), bf16),
            pltpu.VMEM((D, 768), f32),
            pltpu.VMEM((D, 768), bf16),
            pltpu.SemaphoreType.DMA((len(pieces),)),
            pltpu.SemaphoreType.DMA((32,)),
        ),
        compiler_params=pltpu.CompilerParams(vmem_limit_bytes=VMEM_LIMIT),
        cost_estimate=pl.CostEstimate(flops=5 * 10**9, bytes_accessed=8 << 20, transcendentals=0),
        name="decode",
    )(inv_area, encoded, node, hidden, areas, targets, gains, *pieces)


def first_norm_back(layer, gmid, grad_normed, hidden, gain_ref):
    normal, inverse = norm_parts(hidden)
    grad_first, grad_gain = norm_back(grad_normed, normal, inverse, gain_ref[2 * layer : 2 * layer + 1, :])
    return gmid + grad_first, grad_gain


def add_received(fast, own, received):
    if not fast:
        return own[...] + received[0][...].astype(f32)
    by_x, by_y, late_x, late_y = received
    half = own.shape[0] // 2
    top = own[:half, :] + by_x[:half, :].astype(f32) + late_y[...].astype(f32)
    low = own[half:, :] + by_y[:half, :].astype(f32) + late_x[...].astype(f32)
    return jnp.concatenate([top, low], axis=0)


def layer_backward_body(layer, fast, above, pieces, fresh, adj_ref, *refs):
    refs = list(refs)
    take = lambda count: [refs.pop(0) for _ in range(count)]
    if above is None:
        (gh_ref,) = take(1)
    else:
        gmid_above, gown_above, habove_ref = take(3)
        received = take(above)
    mid_ref, att_ref, q_ref, k_ref, v_ref, lse_ref, gain_ref = take(7)
    piece_refs = take(pieces)
    if not fresh:
        take(2)
    gmid_ref, gq_ref, gk_ref, gv_ref, ggain_ref, keep_ref, send_ref = take(7)
    sent = take(4 if fast else 1)
    if above is not None:
        (ggain_above_ref,) = take(1)
    kg, vg, gatt_ref, dk, dv, w_ref, grest_ref, sems, out_sems = refs
    fetched = fetch(piece_refs, w_ref, sems)
    if above is None:
        grad_hidden = gh_ref[...]
    else:
        grad_hidden, ggain_above_ref[...] = first_norm_back(
            layer + 1, gmid_above[...], add_received(fast, gown_above, received), habove_ref[...], gain_ref
        )
    low = grad_hidden.astype(bf16)
    normal, inverse = norm_parts(mid_ref[...])
    gain = gain_ref[2 * layer + 1 : 2 * layer + 2, :]
    normed = (normal * gain).astype(bf16)
    finish(fetched)
    inner = nn(normed, w_ref[:, 4 * D : 5 * D])
    sigma = sigmoid(inner)
    activated = (inner * sigma).astype(bf16)
    grest_ref[:, 2 * D :] = tn(activated, low).astype(bf16)
    grad_act = nt(low, w_ref[:, 5 * D :])
    grad_inner = (grad_act * (sigma * (1.0 + inner * (1.0 - sigma)))).astype(bf16)
    grest_ref[:, D : 2 * D] = tn(normed, grad_inner).astype(bf16)
    grad_normed = nt(grad_inner, w_ref[:, 4 * D : 5 * D])
    grad_mid, ggain_ref[...] = norm_back(grad_normed, normal, inverse, gain)
    grad_mid = grad_hidden + grad_mid
    gmid_ref[...] = grad_mid
    branch = grad_mid.astype(bf16)
    grest_ref[:, :D] = tn(att_ref[...], branch).astype(bf16)
    emitted = emit(fast, grest_ref, keep_ref, send_ref, out_sems, 3 * D, SHARD_ROWS, 32)
    gatt_ref[...] = nt(branch, w_ref[:, 3 * D : 4 * D]).astype(bf16)
    dk[...] = jnp.zeros_like(dk)
    dv[...] = jnp.zeros_like(dv)
    blocks = mid_ref.shape[0] // BLOCK
    turn = lax.axis_index("grp") * blocks if fast else 0

    def one_block(r, _):
        rows = pl.ds(pl.multiple_of(r * BLOCK, BLOCK), BLOCK)
        sources = [
            pl.ds(pl.multiple_of((adj_ref[r * SOURCES + j] ^ turn) * BLOCK, BLOCK), BLOCK)
            for j in range(SOURCES)
        ]
        for j in range(SOURCES):
            kg[j * BLOCK : (j + 1) * BLOCK, :] = k_ref[sources[j], :]
            vg[j * BLOCK : (j + 1) * BLOCK, :] = v_ref[sources[j], :]
        for g in range(D // LANES):
            lanes = slice(g * LANES, (g + 1) * LANES)
            query = spread_heads(q_ref[rows, lanes] * jnp.asarray(score_scale, bf16))
            grad_out = spread_heads(gatt_ref[rows, lanes])
            probs = jnp.exp(nt(kg[:, lanes], query) - lse_ref[r, g, 0:1, :])
            grad_probs = nt(vg[:, lanes], grad_out)
            inner_sum = jnp.sum(probs * grad_probs, axis=0, keepdims=True)
            grad_scores = (probs * (grad_probs - inner_sum)).astype(bf16)
            grad_value = nn(probs.astype(bf16), grad_out)
            grad_key = nn(grad_scores, query)
            grad_query = gather_heads(tn(grad_scores, kg[:, lanes])) * score_scale
            gq_ref[rows, lanes] = grad_query.astype(bf16)
            for j in range(SOURCES):
                dk[sources[j], lanes] += grad_key[j * BLOCK : (j + 1) * BLOCK]
                dv[sources[j], lanes] += grad_value[j * BLOCK : (j + 1) * BLOCK]
        return 0

    lax.fori_loop(0, blocks, one_block, 0)
    for first in range(0, dk.shape[0], 512):
        rows = slice(first, first + 512)
        grad_key = dk[rows, :].astype(bf16)
        grad_value = dv[rows, :].astype(bf16)
        gk_ref[rows, :] = grad_key
        gv_ref[rows, :] = grad_value
        if fast and first == 0:
            continue
        back = (nt(grad_key, w_ref[:, D : 2 * D]) + nt(grad_value, w_ref[:, 2 * D : 3 * D])).astype(bf16)
        if not fast:
            sent[0][rows, :] = back
            continue
        send_x, send_y, hold_x, hold_y = sent
        top, lower = back[:256], back[256:]
        if first == 512:
            send_x[:256, :] = top
            hold_x[...] = lower
        elif first == 1024:
            send_y[:256, :] = lower
            hold_y[...] = top
        else:
            send_x[256:, :] = top
            send_y[256:, :] = lower
    finish(emitted)


def layer_backward(layer, fast, above, adj, mid, att, q, k, v, lse, pieces, gains, grads):
    nodes = mid.shape[0]
    pool = k.shape[0]
    fresh = grads is None
    width = WIDTH_LAYER if fresh else grads[0].shape[2]
    sds = jax.ShapeDtypeStruct
    outs = [
        sds((nodes, D), f32),
        sds((nodes, D), bf16),
        sds((pool, D), bf16),
        sds((pool, D), bf16),
        sds((1, D), f32),
        sds((16, SHARD_ROWS, width), bf16),
        sds((16, SHARD_ROWS, width), bf16),
    ]
    out_specs = [whole()] * 5 + [ANYWHERE] * 2
    if fast:
        outs += [sds((nodes, D), bf16)] * 2 + [sds((nodes // 2, D), bf16)] * 2
        out_specs += [whole()] * 4
    else:
        outs += [sds((pool, D), bf16)]
        out_specs += [whole()]
    count = None if len(above) == 1 else len(above) - 3
    if count is not None:
        outs.append(sds((1, D), f32))
        out_specs.append(whole())
    vmem_ins = len(above) + 7
    aliases = {} if fresh else {1 + vmem_ins + len(pieces): 5, 2 + vmem_ins + len(pieces): 6}
    return call(
        functools.partial(layer_backward_body, layer, fast, count, len(pieces), fresh),
        tuple(outs),
        [whole(pltpu.SMEM)] + [whole()] * vmem_ins + [ANYWHERE] * (len(pieces) + (0 if fresh else 2)),
        scratch=(
            pltpu.VMEM((PICKED, D), bf16),
            pltpu.VMEM((PICKED, D), bf16),
            pltpu.VMEM((nodes, D), bf16),
            pltpu.VMEM((pool, D), f32),
            pltpu.VMEM((pool, D), f32),
            pltpu.VMEM((D, WIDTH_LAYER), bf16),
            pltpu.VMEM((D, 3 * D), bf16),
            pltpu.SemaphoreType.DMA((len(pieces),)),
            pltpu.SemaphoreType.DMA((32,)),
        ),
        flops=12 * 10**9,
        name=f"layer_backward_{layer}",
        out_specs=tuple(out_specs),
        input_output_aliases=aliases,
    )(adj, *above, mid, att, q, k, v, lse, gains, *pieces, *(grads or ()))


def projection_back_body(fast, parts, pieces, own_ref, *refs):
    refs = list(refs)
    take = lambda count: [refs.pop(0) for _ in range(count)]
    part_refs = take(parts)
    gq_ref, gk_ref, gv_ref = take(3)
    piece_refs = take(pieces)
    take(2)
    gown_ref, keep_ref, send_ref = take(3)
    w_ref, gw_ref, sems, out_sems = refs
    fetched = fetch(piece_refs, w_ref, sems)
    gw_ref[:, :D] = tn(own_ref[...], gq_ref[...]).astype(bf16)
    for index, source in ((1, gk_ref), (2, gv_ref)):
        total = None
        start = 0
        for part in part_refs:
            rows = part.shape[0]
            value = tn(part[...], source[start : start + rows, :])
            total = value if total is None else total + value
            start += rows
        gw_ref[:, index * D : (index + 1) * D] = total.astype(bf16)
    emitted = emit(fast, gw_ref, keep_ref, send_ref, out_sems, 0, SHARD_ROWS, 32)
    finish(fetched)
    back = nt(gq_ref[...], w_ref[:, :D])
    if fast:
        rows = own_ref.shape[0]
        back = back + nt(gk_ref[:rows, :], w_ref[:, D : 2 * D]) + nt(gv_ref[:rows, :], w_ref[:, 2 * D :])
    gown_ref[...] = back
    finish(emitted)


def projection_back(layer, fast, own, parts, gq, gk, gv, pieces, grads):
    sds = jax.ShapeDtypeStruct
    grad_shape = sds(grads[0].shape, bf16)
    at = len(parts) + 4 + len(pieces)
    return call(
        functools.partial(projection_back_body, fast, len(parts), len(pieces)),
        (sds((own.shape[0], D), f32), grad_shape, grad_shape),
        [whole()] * (len(parts) + 4) + [ANYWHERE] * (len(pieces) + 2),
        scratch=(
            pltpu.VMEM((D, 3 * D), bf16),
            pltpu.VMEM((D, 3 * D), bf16),
            pltpu.SemaphoreType.DMA((len(pieces),)),
            pltpu.SemaphoreType.DMA((32,)),
        ),
        flops=3 * 10**9,
        name=f"projection_back_{layer}",
        out_specs=(whole(), ANYWHERE, ANYWHERE),
        input_output_aliases={at: 1, at + 1: 2},
    )(own, *parts, gq, gk, gv, *pieces, *grads)


def encode_back_body(fast, parts, gmid_ref, gown_ref, h_ref, *refs):
    received = refs[:parts]
    gain_ref, cells_ref, node_ref, gcomb_ref, count_ref = refs[parts : parts + 5]
    ggains = refs[parts + 5 : parts + 9]
    keep_ref, send_ref, gh_ref, total_ref, low_ref, out_sems = refs[parts + 9 :]
    step = pl.program_id(0)
    c_in = cells_ref.shape[1]

    @pl.when(step == 0)
    def _():
        grad_hidden, grad_gain = first_norm_back(
            0, gmid_ref[...], add_received(fast, gown_ref, received), h_ref[...], gain_ref
        )
        gh_ref[...] = grad_hidden
        stacked = jnp.concatenate(
            [grad_gain] + [g[...] for g in ggains] + [jnp.zeros((BLOCK - 1 - len(ggains), D), f32)], axis=0
        )
        total_ref[...] = jnp.zeros_like(total_ref)
        total_ref[:, GAIN_AT:] = jnp.transpose(stacked)

    rows = pl.ds(pl.multiple_of(step * BLOCK, BLOCK), BLOCK)
    summed = (gh_ref[rows, :] / count_ref[:, :1]).astype(bf16)
    match = node_match(node_ref[0]).astype(bf16)
    grad_enc = (gcomb_ref[...].astype(f32) + tn(match, summed)).astype(bf16)
    total_ref[:, :c_in] += tn(grad_enc, cells_ref[...])

    @pl.when(step == pl.num_programs(0) - 1)
    def _():
        low_ref[...] = total_ref[...].astype(bf16)
        finish(emit(fast, low_ref, keep_ref, send_ref, out_sems, 0, 64, 8))


def encode_back(fast, gmid, gown, hidden, received, gains, cells, node, gcomb, counts, ggains):
    blocks = cells.shape[0] // CELL_BLOCK
    row_spec = lambda rows, cols: pl.BlockSpec((rows, cols), lambda i: (i, 0))
    fixed = lambda a: pl.BlockSpec(a.shape, lambda i: (0,) * a.ndim)
    sds = jax.ShapeDtypeStruct
    return pl.pallas_call(
        functools.partial(encode_back_body, fast, len(received)),
        grid=(blocks,),
        out_shape=(sds((4, 64, WIDTH_IN), bf16),) * 2,
        in_specs=[fixed(gmid), fixed(gown), fixed(hidden)]
        + [fixed(r) for r in received]
        + [
            fixed(gains),
            row_spec(CELL_BLOCK, cells.shape[1]),
            pl.BlockSpec((1, 1, CELL_BLOCK), lambda i: (i, 0, 0)),
            row_spec(CELL_BLOCK, D),
            row_spec(BLOCK, BLOCK),
        ]
        + [fixed(g) for g in ggains],
        out_specs=(ANYWHERE, ANYWHERE),
        scratch_shapes=(
            pltpu.VMEM((blocks * BLOCK, D), f32),
            pltpu.VMEM((D, WIDTH_IN), f32),
            pltpu.VMEM((D, WIDTH_IN), bf16),
            pltpu.SemaphoreType.DMA((8,)),
        ),
        compiler_params=pltpu.CompilerParams(vmem_limit_bytes=VMEM_LIMIT),
        cost_estimate=pl.CostEstimate(flops=10**9, bytes_accessed=8 << 20, transcendentals=0),
        name="encode_back",
    )(gmid, gown, hidden, *received, gains, cells, node, gcomb, counts, *ggains)


def adam_step(gradient, weight, moment, square, factor, first_fix, second_fix, weight_decay):
    clipped = gradient * factor
    first = beta_one * moment + (1.0 - beta_one) * clipped
    second = beta_two * square + (1.0 - beta_two) * clipped * clipped
    delta = -learn_rate * (
        first / first_fix / (jnp.sqrt(second / second_fix) + adam_eps) + weight_decay * weight
    )
    return (delta, first, second)


NEAR_X = [(i, i ^ 1) for i in range(4)]
NEAR_Y = [(i, i ^ 2) for i in range(4)]
CORNER = [(i, i ^ 3) for i in range(4)]
PARTNER = [(i, i ^ 1) for i in range(8)]


def ahead(steps):
    return [(z * 2 + c, ((z + steps) % 4) * 2 + c) for z in range(4) for c in range(2)]


def gather_pieces(fast, shard):
    if not fast:
        return [lax.all_gather(shard, "shd", axis=0, tiled=True)]
    along = [shard] + [lax.ppermute(shard, "shd", ahead(k)) for k in (1, 2, 3)]
    pieces = []
    for piece in along:
        pieces += [piece, lax.ppermute(piece, "shd", PARTNER)]
    return pieces


def exchange_rows(fast, normed):
    if not fast:
        return [lax.all_gather(normed, "grp", axis=0, tiled=True)]
    half = normed.shape[0] // 2
    by_x = lax.ppermute(normed, "grp", NEAR_X)
    by_y = lax.ppermute(normed, "grp", NEAR_Y)
    top = lax.ppermute(by_x[:half], "grp", NEAR_Y)
    low = lax.ppermute(by_y[half:], "grp", NEAR_X)
    return [normed, by_x, by_y, top, low]


def return_rows(fast, sent):
    if not fast:
        return [lax.psum_scatter(sent[0], "grp", scatter_dimension=0, tiled=True)]
    send_x, send_y, hold_x, hold_y = sent
    half = hold_x.shape[0]
    by_x = lax.ppermute(send_x, "grp", NEAR_X)
    by_y = lax.ppermute(send_y, "grp", NEAR_Y)
    late_x = lax.ppermute(plus(hold_x, by_y[half:]), "grp", NEAR_X)
    late_y = lax.ppermute(plus(hold_y, by_x[half:]), "grp", NEAR_Y)
    return [by_x, by_y, late_x, late_y]


def plus(*terms):
    total = terms[0].astype(f32)
    for term in terms[1:]:
        total = total + term.astype(f32)
    return total.astype(terms[0].dtype)


def swap_all(values, axis, routes):
    return [values[0]] + [lax.ppermute(v, axis, route) for v, route in zip(values[1:], routes)]


def reduce_blocks(fast, keep, send):
    cols = keep.shape[2]
    if not fast:
        full = jnp.concatenate([keep, send], axis=0).reshape(D, cols)
        shard = lax.psum_scatter(full, "shd", scatter_dimension=0, tiled=True)
        return lax.psum(shard, "grp").astype(f32)
    both = plus(keep, lax.ppermute(send, "shd", PARTNER))
    if keep.shape[0] == 4:
        parts = swap_all([both[i] for i in range(4)], "shd", [ahead(k) for k in (1, 2, 3)])
        mine = plus(*parts)
        parts = swap_all([mine] * 4, "grp", (NEAR_X, NEAR_Y, CORNER))
        return sum(p.astype(f32) for p in parts)
    parts = swap_all([both[4 * i : 4 * i + 4] for i in range(4)], "grp", (NEAR_X, NEAR_Y, CORNER))
    mine = plus(*parts)
    parts = swap_all([mine[i] for i in range(4)], "shd", [ahead(k) for k in (1, 2, 3)])
    mine = plus(*parts)
    parts = jnp.stack(swap_all([mine] * 4, "grp", (NEAR_X, NEAR_Y, CORNER)))
    order = lax.axis_index("grp") ^ jnp.arange(4)
    return parts[order].reshape(4 * SHARD_ROWS, cols).astype(f32)


def sum_group(fast, value):
    if not fast:
        return lax.psum(value, "grp")
    value = value + lax.ppermute(value, "grp", NEAR_X)
    return value + lax.ppermute(value, "grp", NEAR_Y)


def sum_shards(fast, value):
    if not fast:
        return lax.psum(value, "shd")
    for step in (1, 2, 4):
        value = value + lax.ppermute(value, "shd", [(i, i ^ step) for i in range(8)])
    return value


def local(
    fast,
    cells_in,
    targets,
    cell_areas,
    cell_node,
    adjacency,
    step_count,
    weight_in,
    weight_layer,
    weight_dec,
    norm_gains,
    moment_in,
    moment_layer,
    moment_dec,
    moment_gains,
    square_in,
    square_layer,
    square_dec,
    square_gains,
):
    blocks = adjacency.shape[0]
    c_in, c_out = weight_in.shape[0], targets.shape[1]
    shard_cols = weight_in.shape[1]
    area_part = jnp.sum(cell_areas)
    side = [weight_in.T.astype(bf16), jnp.zeros((shard_cols, GAIN_AT - c_in), bf16), norm_gains.T.astype(bf16)]
    for value in (area_part // 256, area_part % 256):
        side.append(jnp.broadcast_to(value.astype(bf16), (shard_cols, 1)))
    side.append(jnp.zeros((shard_cols, WIDTH_IN - AREA_AT - 2), bf16))
    low_in = gather_pieces(fast, jnp.concatenate(side, axis=1))
    low_first = gather_pieces(fast, weight_layer[0].astype(bf16))
    top = jnp.concatenate(
        [weight_layer[1], jnp.pad(weight_dec, ((0, 0), (0, WIDTH_TOP - WIDTH_LAYER - D - c_out)))], axis=1
    )
    low_top = gather_pieces(fast, top.astype(bf16))
    low_layer = [low_first, low_top]
    node = cell_node.reshape(blocks, 1, CELL_BLOCK)
    areas = cell_areas.reshape(blocks, 1, CELL_BLOCK)
    adj = adjacency.reshape(-1)
    encoded, hidden, normed, counts, gains, area_shards = encode(cells_in, node, low_in)
    if not fast:
        area_shards = lax.psum(area_part.astype(f32), "shd").reshape(1, 1)
    inv_area = 1.0 / sum_group(fast, area_shards)[0]
    kept = []
    for layer in range(LAYERS):
        parts = exchange_rows(fast, normed)
        out = layer_forward(layer, fast, normed, parts, adj, hidden, low_layer[layer], gains)
        kept.append((hidden, normed, parts) + tuple(out[1:3]) + tuple(out[4:]))
        hidden, normed = out[0], out[3]
    loss_part, gcomb, ghid, gain_dec, *grads = decode(
        fast, inv_area, encoded, node, hidden, areas, targets, low_top, gains
    )
    gain_grads = [None] * (2 * LAYERS + 1)
    gain_grads[2 * LAYERS] = gain_dec
    layer_grads = [None] * LAYERS
    above = (ghid,)
    for layer in reversed(range(LAYERS)):
        h_in, normed, parts, mid, att, q, k, v, lse = kept[layer]
        back = layer_backward(
            layer, fast, above, adj, mid, att, q, k, v, lse, low_layer[layer], gains, grads
        )
        gmid, gq, gk, gv, gain_grads[2 * layer + 1], keep, send = back[:7]
        sent = back[7 : 11 if fast else 8]
        if len(above) > 1:
            gain_grads[2 * layer + 2] = back[-1]
        received = return_rows(fast, sent)
        gown, *grads = projection_back(
            layer, fast, normed, parts, gq, gk, gv, low_layer[layer], (keep, send)
        )
        above = (gmid, gown, h_in, *received)
        layer_grads[layer] = reduce_blocks(fast, *grads)
        grads = None
    gmid, gown, h_in, *received = above
    keep, send = encode_back(
        fast, gmid, gown, h_in, received, gains, cells_in, node, gcomb, counts, gain_grads[1:]
    )
    first_grads = reduce_blocks(fast, keep, send)
    loss_group = sum_group(fast, loss_part)
    group_sums = (
        first_grads[:, :c_in].T,
        jnp.stack([layer_grads[0], layer_grads[1][:, :WIDTH_LAYER]], axis=0),
        layer_grads[1][:, WIDTH_LAYER : WIDTH_LAYER + D + c_out],
        first_grads[:, GAIN_AT : GAIN_AT + 2 * LAYERS + 1].T,
    )
    squares_part = f32(0.0)
    for index_w in range(4):
        squares_part = squares_part + jnp.sum(group_sums[index_w] * group_sums[index_w])
    both = sum_shards(fast, jnp.stack([squares_part, loss_group[0, 0]]))
    total_squares, loss_value = both[0], both[1]
    grad_norm = jnp.sqrt(total_squares)
    factor = clip_limit / jnp.maximum(grad_norm, clip_limit)
    step_value = step_count[0].astype(f32)
    first_fix = 1.0 - jnp.power(f32(beta_one), step_value)
    second_fix = 1.0 - jnp.power(f32(beta_two), step_value)
    weights = (weight_in, weight_layer, weight_dec, norm_gains)
    moments = (moment_in, moment_layer, moment_dec, moment_gains)
    squared = (square_in, square_layer, square_dec, square_gains)
    decays = (decay_coef, decay_coef, decay_coef, 0.0)
    deltas, firsts, seconds = ([], [], [])
    for index_w in range(4):
        delta, first, second = adam_step(
            group_sums[index_w],
            weights[index_w],
            moments[index_w],
            squared[index_w],
            factor,
            first_fix,
            second_fix,
            decays[index_w],
        )
        deltas.append(delta)
        firsts.append(first)
        seconds.append(second)
    return (loss_value, grad_norm, *deltas, *firsts, *seconds)


def solution(mesh):
    rows = P(("grp", "shd"), None)
    flat = P(("grp", "shd"))
    params = (P(None, "shd"), P(None, "shd", None), P("shd", None), P(None, "shd"))
    fast = (mesh.shape["grp"], mesh.shape["shd"]) == (4, 8)
    return jax.shard_map(
        functools.partial(local, fast),
        mesh=mesh,
        in_specs=(rows, rows, flat, flat, rows, P()) + params * 3,
        out_specs=(P(), P()) + params * 3,
        check_vma=False,
    )
```
